512 devices in a mesh: row: 16 (over x, z_lo), col: 32 (over y, z_hi, core).
Axes of the slice: x: 4, y: 4, z: 16 (z_hi: 4, z_lo: 4; z = z_hi * 4 + z_lo), core: 2. Of those that a mesh axis runs over, the one named last changes fastest.
Arguments:
- probes: bfloat16 [32, 262144], P(None, ('row', 'col')), may hold values from -6 to 6
- tiles: bfloat16 [16, 32, 9, 512, 512], P('row', 'col'), may hold values from -0.09375 to 0.09375
- tile_index: int32 [16, 32, 9, 2], P('row', 'col'), may hold values from 0 to 31, as said below
- tile_count: int32 [16, 32], P('row', 'col'), may hold values from 2 to 9, as said below
- coefficients: float32 [5], replicated, may hold values from 0.2 to 1
Outputs:
- heat: float32 [32, 262144], P(None, ('row', 'col'))
The draws below stay inside these ranges and needn't reach their ends.
Inputs may be any that keep to these rules, and one draw needn't show every extreme that they name: `tile_index`: on each device the 9 slots name distinct positions (local block row below 32, local block column below 16); slot 0 is the tile whose block row and block column are both the first block of the device's own probe segment. `tile_count`: at least one device holds exactly 9 live slots.
All inputs are finite; a program needn't handle non-finite values.
Results may differ from the reference program's by a relative error of at most 0.029.
Values may be sent and summed in bfloat16 or wider, within the bound.
No kernel may reach another device: no remote copies, remote signals or barrier semaphores. Data moves between devices by JAX's collectives and lax.ppermute only.
A program may use at most 64 MiB of HBM per device.

```python
import math
import jax
import jax.numpy as jnp
from jax import lax

TILE = 512
PROBES = 32
ITERS = 4
SEG_BLK = 1
TMAX = 9
NODES = 262144
N_ROW = 16
N_COL = 32


def pattern_draw(key):
    base = jax.random.fold_in(key, 11)
    keys = jax.random.split(base, 4)
    across = N_ROW * SEG_BLK
    places = N_COL * SEG_BLK * across
    top_score = max(2, 2 ** 30 // places)
    positions = jnp.arange(places, dtype=jnp.int32)
    scores = jax.random.randint(keys[0], (N_ROW, N_COL, places), 0, top_score, dtype=jnp.int32) * places + positions
    grid_rows = jnp.arange(N_ROW, dtype=jnp.int32)[:, None]
    grid_cols = jnp.arange(N_COL, dtype=jnp.int32)[None, :]
    own_place = grid_cols * SEG_BLK * across + grid_rows * SEG_BLK
    scores = jnp.where(positions[None, None, :] == own_place[:, :, None], -1, scores)
    chosen = jnp.argsort(scores, axis=-1)[..., :TMAX].astype(jnp.int32)
    index = jnp.stack([chosen // across, chosen % across], axis=-1).astype(jnp.int32)
    lowest = max(2, TMAX // 2)
    counts = jax.random.randint(keys[1], (N_ROW, N_COL), lowest, TMAX + 1, dtype=jnp.int32)
    fullest = jax.random.randint(keys[3], (), 0, N_ROW * N_COL, dtype=jnp.int32)
    flat = jnp.arange(N_ROW * N_COL, dtype=jnp.int32).reshape(N_ROW, N_COL)
    counts = jnp.where(flat == fullest, TMAX, counts).astype(jnp.int32)
    return (index, counts)


def draw_tile_index(key, part):
    index, counts = pattern_draw(key)
    return index


def draw_tile_count(key, part):
    index, counts = pattern_draw(key)
    return counts


def block_levels(stream_key, shape, pieces, low, largest):
    factor_of, own = 1.0, jax.random.fold_in(stream_key, 6)
    for axis_at, parts in pieces:
        draws = jnp.exp(jax.random.uniform(jax.random.fold_in(own, axis_at), (parts,), jnp.float32, low / len(pieces), largest / len(pieces)))
        factor_of = factor_of * jnp.repeat(draws, shape[axis_at] // parts).reshape([-1 if axis == axis_at else 1 for axis in range(len(shape))])
    return factor_of


def noise(key, extent, scale, bound, cuts=(), kind=jnp.bfloat16):
    array = jax.random.normal(key, extent, jnp.float32) * scale
    if len(cuts) > 0:
        array = block_levels(key, extent, cuts, -0.22, 0.18) * array
    return jnp.clip(array, min=-bound, max=bound).astype(kind)


def setup_inputs(seed: int = 0) -> dict:
    seeds = jax.random.split(jax.random.key(seed), 6)
    return {
        "probes": noise(seeds[0], (PROBES, NODES), 1.0, 6.0, ((1, 512),)),
        "tiles": noise(seeds[1], (N_ROW, N_COL, TMAX, TILE, TILE), (8 * TILE) ** -0.5, 0.09375, ((0, 16), (1, 32))),
        "tile_index": draw_tile_index(jax.random.fold_in(seeds[5], 71), 0),
        "tile_count": draw_tile_count(jax.random.fold_in(seeds[5], 71), 0),
        "coefficients": jnp.clip(jnp.exp(jax.random.uniform(seeds[4], (ITERS + 1,), jnp.float32, math.log(0.2), math.log(1.0))), 0.2, 1.0),
    }


def apply_operator(field_bf, tiles, tile_index, tile_count):
    width = field_bf.shape[0]
    blocks = field_bf.reshape(width, -1, TILE)
    row_blocks = N_COL * SEG_BLK

    def device_term(number, totals):
        number = jnp.asarray(number).astype(jnp.int32)
        grid_row = number // N_COL
        grid_col = number % N_COL

        def add_slot(slot, partial_value):
            slot = jnp.asarray(slot).astype(jnp.int32)
            one_tile = tiles[grid_row, grid_col, slot]
            row_at = tile_index[grid_row, grid_col, slot, 0].astype(jnp.int32)
            col_at = tile_index[grid_row, grid_col, slot, 1].astype(jnp.int32)
            global_col = ((col_at // SEG_BLK) * N_COL + grid_col) * SEG_BLK + col_at % SEG_BLK
            inputs = lax.dynamic_index_in_dim(blocks, global_col, 1, keepdims=False)
            product = jnp.dot(inputs, one_tile.T, preferred_element_type=jnp.float32)
            in_use = (slot < tile_count[grid_row, grid_col]).astype(jnp.float32)
            earlier = lax.dynamic_index_in_dim(partial_value, row_at, 1, keepdims=False)
            return lax.dynamic_update_index_in_dim(partial_value, earlier + in_use * product, row_at, 1)

        partial_value = lax.fori_loop(0, TMAX, add_slot, jnp.zeros((width, row_blocks, TILE), jnp.float32))
        rounded = lax.optimization_barrier(partial_value.astype(jnp.bfloat16)).astype(jnp.float32)
        start = (grid_row * row_blocks).astype(jnp.int32)
        earlier = lax.dynamic_slice_in_dim(totals, start, row_blocks, 1)
        return lax.dynamic_update_slice_in_dim(totals, earlier + rounded, start, 1)

    totals = lax.fori_loop(0, N_ROW * N_COL, device_term, jnp.zeros((width, blocks.shape[1], TILE), jnp.float32))
    return totals.reshape(width, -1)


def reference(probes, tiles, tile_index, tile_count, coefficients):
    previous = probes.astype(jnp.float32)
    current = apply_operator(probes, tiles, tile_index, tile_count)
    heat = coefficients[0] * previous + coefficients[1] * current
    for order in range(2, ITERS + 1):
        following = 2.0 * apply_operator(current.astype(jnp.bfloat16), tiles, tile_index, tile_count) - previous
        previous, current = current, following
        heat = heat + coefficients[order] * following
    return heat
```

```python
import jax
import jax.numpy as jnp
from jax import lax
from jax.experimental import pallas as pl
from jax.experimental.pallas import tpu as pltpu
from jax.sharding import Mesh, PartitionSpec as P

TILE = 512
ITERS = 4
AXES = ("x", "zl", "y", "zh", "c")
SIZES = (4, 4, 4, 4, 2)


def tile_kernel(index_ref, count_ref, core_ref, panel_ref, tiles_ref, mine_ref, theirs_ref, acc_ref):
    acc_ref[...] = jnp.zeros_like(acc_ref)
    count = count_ref[0]
    core = core_ref[0]
    for slot in range(tiles_ref.shape[0]):
        row = index_ref[2 * slot]
        col = index_ref[2 * slot + 1]
        picked = panel_ref[col]
        picked = jnp.where(slot < count, picked, jnp.zeros_like(picked))
        product = lax.dot_general(
            picked, tiles_ref[slot], (((1,), (1,)), ((), ())), preferred_element_type=jnp.float32
        )
        away = (row % 2) ^ core
        at = away * 16 + row // 2
        acc_ref[at] += product
    mine_ref[...] = acc_ref[:16].astype(jnp.bfloat16)
    theirs_ref[...] = acc_ref[16:].astype(jnp.bfloat16)


def on_device(probes, tiles, tile_index, tile_count, coefficients):
    width = probes.shape[0]
    slabs = tiles[0, 0]
    index = tile_index[0, 0].reshape(-1)
    count = tile_count[0]
    core = lax.axis_index("c").astype(jnp.int32).reshape(1)
    smem = pl.BlockSpec(memory_space=pltpu.SMEM)
    vmem = pl.BlockSpec(memory_space=pltpu.VMEM)
    half = jax.ShapeDtypeStruct((16, width, TILE), jnp.bfloat16)
    multiply = pl.pallas_call(
        tile_kernel,
        out_shape=(half, half),
        in_specs=[smem, smem, smem, vmem, vmem],
        out_specs=(vmem, vmem),
        scratch_shapes=[pltpu.VMEM((32, width, TILE), jnp.float32)],
        compiler_params=pltpu.CompilerParams(vmem_limit_bytes=32 * 1024 * 1024),
        name="tiles",
    )

    def spread(field, axis):
        copies = jnp.broadcast_to(field[None], (4,) + field.shape)
        return lax.all_to_all(copies, axis, 0, 0, tiled=True)

    def total(parts, axis):
        arrived = lax.all_to_all(parts, axis, 0, 0, tiled=True)
        return jnp.sum(arrived.astype(jnp.float32), axis=0)

    def operate(field_bf):
        panel = spread(spread(field_bf, "zl"), "x").reshape(16, width, TILE)
        mine, theirs = multiply(index, count, core, panel, slabs)
        other = lax.ppermute(theirs, "c", [(0, 1), (1, 0)])
        chip = (mine.astype(jnp.float32) + other.astype(jnp.float32)).astype(jnp.bfloat16)
        along_y = total(chip.reshape(4, 4, width, TILE), "y").astype(jnp.bfloat16)
        return total(along_y, "zh")

    previous = probes.astype(jnp.float32)
    current = operate(probes)
    heat = coefficients[0] * previous + coefficients[1] * current
    for order in range(2, ITERS + 1):
        following = 2.0 * operate(current.astype(jnp.bfloat16)) - previous
        previous, current = (current, following)
        heat = heat + coefficients[order] * following
    return heat


def solution(mesh):
    physical = Mesh(mesh.devices.reshape(SIZES), AXES)
    row, col = AXES[:2], AXES[2:]
    return jax.shard_map(
        on_device,
        mesh=physical,
        in_specs=(
            P(None, AXES),
            P(row, col, None, None, None),
            P(row, col, None, None),
            P(row, col),
            P(),
        ),
        out_specs=P(None, AXES),
        check_vma=False,
    )
```

```python
import jax
import jax.numpy as jnp
from jax import lax
from jax.experimental import pallas as pl
from jax.experimental.pallas import tpu as pltpu
from jax.sharding import Mesh, PartitionSpec as P

TILE = 512
AXES = ("x", "zl", "y", "zh", "c")
SIZES = (4, 4, 4, 4, 2)
SMEM = pl.BlockSpec(memory_space=pltpu.SMEM)
VMEM = pl.BlockSpec(memory_space=pltpu.VMEM)
SWAP = [(0, 1), (1, 0)]
CORE = 0
OWN = 1
OTHER = 20


def tile_kernel(table_ref, panel_ref, own_ref, other_ref, partial_ref, acc_ref):
    acc_ref[...] = jnp.zeros_like(acc_ref)
    core = table_ref[CORE]
    slots = own_ref.shape[0]
    for tiles_ref, start, parity in ((own_ref, OWN, core), (other_ref, OTHER, 1 - core)):
        for slot in range(slots):
            row = table_ref[start + 2 * slot]
            col = table_ref[start + 2 * slot + 1]
            picked = panel_ref[col, parity]
            picked = jnp.where(slot < table_ref[start + 2 * slots], picked, jnp.zeros_like(picked))
            acc_ref[row] += lax.dot_general(
                picked, tiles_ref[slot], (((1,), (1,)), ((), ())), preferred_element_type=jnp.float32
            )
    partial_ref[...] = acc_ref[...].astype(jnp.bfloat16)


def last_kernel(
    table_ref,
    weight_ref,
    panel_ref,
    own_ref,
    other_ref,
    t0_ref,
    t1_ref,
    t2_ref,
    t3_ref,
    partial_ref,
    base_ref,
    scale_ref,
    acc_ref,
):
    base_ref[...] = (
        weight_ref[0] * t0_ref[...].astype(jnp.float32)
        + weight_ref[1] * t1_ref[...]
        + (weight_ref[2] - weight_ref[4]) * t2_ref[...]
        + weight_ref[3] * t3_ref[...]
    )
    scale_ref[...] = jnp.full(scale_ref.shape, 2.0 * weight_ref[4], jnp.float32)
    tile_kernel(table_ref, panel_ref, own_ref, other_ref, partial_ref, acc_ref)


def on_device(probes, tiles, tile_index, tile_count, coefficients):
    slabs = tiles[0, 0]
    half = probes.shape[0] // 2
    core = lax.axis_index("c").astype(jnp.int32)
    first = core == 0

    def ordered(mine, its):
        return jnp.where(first, jnp.stack([mine, its]), jnp.stack([its, mine]))

    keep = jnp.where(first, probes[:half], probes[half:])
    give = jnp.where(first, probes[half:], probes[:half])
    note = jnp.concatenate([tile_index[0, 0].reshape(-1), tile_count[0]])
    flat = jnp.pad(note.astype(jnp.bfloat16), (0, half * TILE - note.shape[0])).reshape(half, TILE)
    arrived = lax.ppermute(jnp.concatenate([give, flat]), "c", SWAP)
    field = ordered(keep, arrived[:half])
    table = jnp.concatenate([core.reshape(1), note, arrived[half, : note.shape[0]].astype(jnp.int32)])
    field, table, slabs = lax.optimization_barrier((field, table, slabs))
    others = lax.ppermute(slabs, "c", SWAP)

    rows = SIZES[2] * SIZES[3] * SIZES[4]
    partial = jax.ShapeDtypeStruct((rows, half, TILE), jnp.bfloat16)
    plane = jax.ShapeDtypeStruct((2, half, TILE), jnp.float32)
    acc = pltpu.VMEM(partial.shape, jnp.float32)
    params = pltpu.CompilerParams(vmem_limit_bytes=4 * 1024 * 1024)

    def gather(field_bf):
        copies = jnp.broadcast_to(field_bf[None], (SIZES[0] * SIZES[1],) + field_bf.shape)
        return lax.all_to_all(copies, ("x", "zl"), 0, 0, tiled=True)

    def total(parts, axis):
        arrived = lax.all_to_all(parts, axis, 0, 0, tiled=True).astype(jnp.float32)
        return (arrived[0] + arrived[1]) + (arrived[2] + arrived[3])

    def reduce(part):
        along_y = total(part.reshape(SIZES[2], -1, half, TILE), "y").astype(jnp.bfloat16)
        return total(along_y.reshape(SIZES[3], 2, half, TILE), "zh")

    following = pl.pallas_call(
        tile_kernel,
        out_shape=partial,
        in_specs=[SMEM, VMEM, VMEM, VMEM],
        out_specs=VMEM,
        scratch_shapes=[acc],
        compiler_params=params,
        name="tiles",
    )
    t1 = reduce(following(table, gather(field), slabs, others))
    t2 = 2.0 * reduce(following(table, gather(t1.astype(jnp.bfloat16)), slabs, others)) - field.astype(jnp.float32)
    t3 = 2.0 * reduce(following(table, gather(t2.astype(jnp.bfloat16)), slabs, others)) - t1

    part, base, scale = pl.pallas_call(
        last_kernel,
        out_shape=(partial, plane, plane),
        in_specs=[SMEM, SMEM] + [VMEM] * 7,
        out_specs=(VMEM, VMEM, VMEM),
        scratch_shapes=[acc],
        compiler_params=params,
        name="last",
    )(table, coefficients, gather(t3.astype(jnp.bfloat16)), slabs, others, field, t1, t2, t3)
    heat = base + scale * reduce(part)

    mine = jnp.where(first, heat[0], heat[1])
    its = lax.ppermute(jnp.where(first, heat[1], heat[0]), "c", SWAP)
    return ordered(mine, its).reshape(2 * half, TILE)


def solution(mesh):
    physical = Mesh(mesh.devices.reshape(SIZES), AXES)
    row, col = AXES[:2], AXES[2:]
    return jax.shard_map(
        on_device,
        mesh=physical,
        in_specs=(
            P(None, AXES),
            P(row, col, None, None, None),
            P(row, col, None, None),
            P(row, col),
            P(),
        ),
        out_specs=P(None, AXES),
        check_vma=False,
    )
```

```python
import jax
import jax.numpy as jnp
from jax import lax
from jax.experimental import pallas as pl
from jax.experimental.pallas import tpu as pltpu
from jax.sharding import Mesh, PartitionSpec as P

TILE = 512
AXES = ("x", "zl", "y", "zh", "c")
SIZES = (4, 4, 4, 4, 2)
SMEM = pl.BlockSpec(memory_space=pltpu.SMEM)
VMEM = pl.BlockSpec(memory_space=pltpu.VMEM)
SWAP = [(0, 1), (1, 0)]
ROW, COL, COUNT, CORE, NOTE = 0, 1, 2, 3, 4


def add_tiles(table_ref, panel_ref, groups, partial_ref, acc_ref):
    acc_ref[...] = jnp.zeros_like(acc_ref)
    for note, slots, tile_of in groups:
        parity = table_ref[note + CORE, 0]
        for slot in range(slots):
            row = table_ref[note + ROW, slot]
            col = table_ref[note + COL, slot]
            picked = panel_ref[col % SIZES[1], col // SIZES[1], parity]
            picked = jnp.where(slot < table_ref[note + COUNT, 0], picked, jnp.zeros_like(picked))
            acc_ref[row] += lax.dot_general(
                picked, tile_of(slot), (((1,), (1,)), ((), ())), preferred_element_type=jnp.float32
            )
    partial_ref[...] = acc_ref[...].astype(jnp.bfloat16)


def first_kernel(table_ref, panel_ref, own_ref, other_ref, partial_ref, acc_ref, held_ref, sems):
    slots = own_ref.shape[0]
    copies = [pltpu.make_async_copy(own_ref.at[slot], held_ref.at[slot], sems.at[slot]) for slot in range(slots)]
    for copy in copies:
        copy.start()

    def held(slot):
        copies[slot].wait()
        return held_ref[slot]

    groups = (NOTE, slots, lambda slot: other_ref[slot]), (0, slots, held)
    add_tiles(table_ref, panel_ref, groups, partial_ref, acc_ref)


def tile_kernel(table_ref, panel_ref, own_ref, other_ref, partial_ref, acc_ref):
    slots = own_ref.shape[0]
    groups = (NOTE, slots, lambda slot: other_ref[slot]), (0, slots, lambda slot: own_ref[slot])
    add_tiles(table_ref, panel_ref, groups, partial_ref, acc_ref)


def last_kernel(
    table_ref,
    weight_ref,
    panel_ref,
    own_ref,
    other_ref,
    t0_ref,
    t1_ref,
    t2_ref,
    t3_ref,
    partial_ref,
    base_ref,
    scale_ref,
    acc_ref,
):
    base_ref[...] = (
        weight_ref[0] * t0_ref[...].astype(jnp.float32)
        + weight_ref[1] * t1_ref[...]
        + (weight_ref[2] - weight_ref[4]) * t2_ref[...]
        + weight_ref[3] * t3_ref[...]
    )
    scale_ref[...] = jnp.full(scale_ref.shape, 2.0 * weight_ref[4], jnp.float32)
    tile_kernel(table_ref, panel_ref, own_ref, other_ref, partial_ref, acc_ref)


def on_device(probes, tiles, tile_index, tile_count, coefficients):
    slabs = tiles[0, 0]
    half = probes.shape[0] // 2
    core = lax.axis_index("c").astype(jnp.int32)
    first = core == 0

    def ordered(mine, its):
        return jnp.where(first, jnp.stack([mine, its]), jnp.stack([its, mine]))

    keep = jnp.where(first, probes[:half], probes[half:])
    give = jnp.where(first, probes[half:], probes[:half])
    slots = slabs.shape[0]
    note = jnp.concatenate(
        [
            tile_index[0, 0].T,
            jnp.broadcast_to(tile_count, (1, slots)),
            jnp.broadcast_to(core, (1, slots)),
        ]
    ).astype(jnp.bfloat16)
    send = jnp.concatenate([give, jnp.pad(note, ((0, half - NOTE), (0, TILE - slots)))])
    arrived = lax.ppermute(send, "c", SWAP)
    field = ordered(keep, arrived[:half])
    table = jnp.concatenate([note, arrived[half : half + NOTE, :slots]]).astype(jnp.int32)
    field, table, slabs = lax.optimization_barrier((field, table, slabs))
    others = lax.ppermute(slabs, "c", SWAP)

    rows = SIZES[2] * SIZES[3] * SIZES[4]
    partial = jax.ShapeDtypeStruct((rows, half, TILE), jnp.bfloat16)
    plane = jax.ShapeDtypeStruct((2, half, TILE), jnp.float32)
    acc = pltpu.VMEM(partial.shape, jnp.float32)
    params = pltpu.CompilerParams(vmem_limit_bytes=4 * 1024 * 1024)

    def gather(field_bf):
        copies = jnp.broadcast_to(field_bf[None], (SIZES[1] * SIZES[0],) + field_bf.shape)
        panel = lax.all_to_all(copies, ("zl", "x"), 0, 0, tiled=True)
        return panel.reshape((SIZES[1], SIZES[0]) + field_bf.shape)

    def total(parts, axis):
        arrived = lax.all_to_all(parts, axis, 0, 0, tiled=True)
        a, b, c, d = (arrived[k].astype(jnp.float32) for k in range(4))
        return (a + b) + (c + d)

    def reduce(part):
        along_y = total(part.reshape(SIZES[2], -1, half, TILE), "y").astype(jnp.bfloat16)
        return total(along_y.reshape(SIZES[3], 2, half, TILE), "zh")

    t1 = reduce(
        pl.pallas_call(
            first_kernel,
            out_shape=partial,
            in_specs=[SMEM, VMEM, pl.BlockSpec(memory_space=pltpu.HBM), VMEM],
            out_specs=VMEM,
            scratch_shapes=[acc, pltpu.VMEM(slabs.shape, slabs.dtype), pltpu.SemaphoreType.DMA((slots,))],
            compiler_params=pltpu.CompilerParams(vmem_limit_bytes=16 * 1024 * 1024),
            name="first",
        )(table, gather(field), pltpu.with_memory_space_constraint(slabs, pltpu.HBM), others)
    )
    following = pl.pallas_call(
        tile_kernel,
        out_shape=partial,
        in_specs=[SMEM, VMEM, VMEM, VMEM],
        out_specs=VMEM,
        scratch_shapes=[acc],
        compiler_params=params,
        name="tiles",
    )

    def settled(value):
        return lax.optimization_barrier((value, value.astype(jnp.bfloat16)))

    t1, field_1 = settled(t1)
    t2 = 2.0 * reduce(following(table, gather(field_1), slabs, others)) - field.astype(jnp.float32)
    t2, field_2 = settled(t2)
    t3 = 2.0 * reduce(following(table, gather(field_2), slabs, others)) - t1
    t3, field_3 = settled(t3)

    part, base, scale = pl.pallas_call(
        last_kernel,
        out_shape=(partial, plane, plane),
        in_specs=[SMEM, SMEM] + [VMEM] * 7,
        out_specs=(VMEM, VMEM, VMEM),
        scratch_shapes=[acc],
        compiler_params=params,
        name="last",
    )(table, coefficients, gather(field_3), slabs, others, field, t1, t2, t3)
    heat = base + scale * reduce(part)

    mine = jnp.where(first, heat[0], heat[1])
    its = lax.ppermute(jnp.where(first, heat[1], heat[0]), "c", SWAP)
    return ordered(mine, its).reshape(2 * half, TILE)


def solution(mesh):
    physical = Mesh(mesh.devices.reshape(SIZES), AXES)
    row, col = AXES[:2], AXES[2:]
    return jax.shard_map(
        on_device,
        mesh=physical,
        in_specs=(
            P(None, AXES),
            P(row, col, None, None, None),
            P(row, col, None, None),
            P(row, col),
            P(),
        ),
        out_specs=P(None, AXES),
        check_vma=False,
    )
```

```python
import jax
import jax.numpy as jnp
from jax import lax
from jax.experimental import pallas as pl
from jax.experimental.pallas import tpu as pltpu
from jax.sharding import Mesh, PartitionSpec as P

TILE = 512
AXES = ("x", "zl", "y", "zh", "c")
SIZES = (4, 4, 4, 4, 2)
SMEM = pl.BlockSpec(memory_space=pltpu.SMEM)
VMEM = pl.BlockSpec(memory_space=pltpu.VMEM)
SWAP = [(0, 1), (1, 0)]
ROW, COL, COUNT, CORE, NOTE = 0, 1, 2, 3, 4


def add_tiles(table_ref, panel_ref, groups, partial_ref, acc_ref):
    acc_ref[...] = jnp.zeros_like(acc_ref)
    for note, slots, tile_of in groups:
        parity = table_ref[note + CORE, 0]
        for slot in range(slots):
            row = table_ref[note + ROW, slot]
            col = table_ref[note + COL, slot]
            picked = panel_ref[col % SIZES[1], col // SIZES[1], parity]
            picked = jnp.where(slot < table_ref[note + COUNT, 0], picked, jnp.zeros_like(picked))
            acc_ref[row] += lax.dot_general(
                picked, tile_of(slot), (((1,), (1,)), ((), ())), preferred_element_type=jnp.float32
            )
    partial_ref[...] = acc_ref[...].astype(jnp.bfloat16)


def first_kernel(table_ref, panel_ref, own_ref, other_ref, partial_ref, held_ref, acc_ref, sems):
    slots = own_ref.shape[0]
    copies = [pltpu.make_async_copy(own_ref.at[slot], held_ref.at[slot], sems.at[slot]) for slot in range(slots)]
    for copy in copies:
        copy.start()

    def held(slot):
        copies[slot].wait()
        return held_ref[slot]

    groups = (NOTE, slots, lambda slot: other_ref[slot]), (0, slots, held)
    add_tiles(table_ref, panel_ref, groups, partial_ref, acc_ref)


def tile_kernel(table_ref, panel_ref, own_ref, other_ref, partial_ref, acc_ref):
    slots = own_ref.shape[0]
    groups = (NOTE, slots, lambda slot: other_ref[slot]), (0, slots, lambda slot: own_ref[slot])
    add_tiles(table_ref, panel_ref, groups, partial_ref, acc_ref)


def last_kernel(
    table_ref,
    weight_ref,
    panel_ref,
    own_ref,
    other_ref,
    t0_ref,
    t1_ref,
    t2_ref,
    t3_ref,
    partial_ref,
    base_ref,
    scale_ref,
    acc_ref,
):
    base_ref[...] = (
        weight_ref[0] * t0_ref[...].astype(jnp.float32)
        + weight_ref[1] * t1_ref[...]
        + (weight_ref[2] - weight_ref[4]) * t2_ref[...]
        + weight_ref[3] * t3_ref[...]
    )
    scale_ref[...] = jnp.full(scale_ref.shape, 2.0 * weight_ref[4], jnp.float32)
    tile_kernel(table_ref, panel_ref, own_ref, other_ref, partial_ref, acc_ref)


def on_device(probes, tiles, tile_index, tile_count, coefficients):
    slabs = tiles[0, 0]
    half = probes.shape[0] // 2
    core = lax.axis_index("c").astype(jnp.int32)
    first = core == 0

    def ordered(mine, its):
        return jnp.where(first, jnp.stack([mine, its]), jnp.stack([its, mine]))

    keep = jnp.where(first, probes[:half], probes[half:])
    give = jnp.where(first, probes[half:], probes[:half])
    slots = slabs.shape[0]
    note = jnp.concatenate(
        [
            tile_index[0, 0].T,
            jnp.broadcast_to(tile_count, (1, slots)),
            jnp.broadcast_to(core, (1, slots)),
        ]
    ).astype(jnp.bfloat16)
    send = jnp.concatenate([give, jnp.pad(note, ((0, half - NOTE), (0, TILE - slots)))])
    send = lax.optimization_barrier(send)
    arrived = lax.ppermute(send, "c", SWAP)
    field = ordered(keep, arrived[:half])
    notes = [both[half : half + NOTE, :slots] for both in (send, arrived)]
    table = jnp.concatenate(notes).astype(jnp.int32)
    field, table, slabs = lax.optimization_barrier((field, table, slabs))
    others = lax.ppermute(slabs, "c", SWAP)

    rows = SIZES[2] * SIZES[3] * SIZES[4]
    partial = jax.ShapeDtypeStruct((rows, half, TILE), jnp.bfloat16)
    plane = jax.ShapeDtypeStruct((2, half, TILE), jnp.float32)
    acc = pltpu.VMEM(partial.shape, jnp.float32)
    params = pltpu.CompilerParams(vmem_limit_bytes=4 * 1024 * 1024)

    def gather(field_bf):
        copies = jnp.broadcast_to(field_bf[None], (SIZES[1] * SIZES[0],) + field_bf.shape)
        panel = lax.all_to_all(copies, ("zl", "x"), 0, 0, tiled=True)
        return panel.reshape((SIZES[1], SIZES[0]) + field_bf.shape)

    def total(parts, axis):
        arrived = lax.all_to_all(parts, axis, 0, 0, tiled=True)
        a, b, c, d = (arrived[k].astype(jnp.float32) for k in range(4))
        return (a + b) + (c + d)

    def reduce(part):
        along_y = total(part.reshape(SIZES[2], -1, half, TILE), "y").astype(jnp.bfloat16)
        return total(along_y.reshape(SIZES[3], 2, half, TILE), "zh")

    part, held = pl.pallas_call(
        first_kernel,
        out_shape=(partial, jax.ShapeDtypeStruct(slabs.shape, slabs.dtype)),
        in_specs=[SMEM, VMEM, pl.BlockSpec(memory_space=pltpu.HBM), VMEM],
        out_specs=(VMEM, VMEM),
        scratch_shapes=[acc, pltpu.SemaphoreType.DMA((slots,))],
        compiler_params=params,
        name="first",
    )(table, gather(field), pltpu.with_memory_space_constraint(slabs, pltpu.HBM), others)
    t1 = reduce(part)
    following = pl.pallas_call(
        tile_kernel,
        out_shape=partial,
        in_specs=[SMEM, VMEM, VMEM, VMEM],
        out_specs=VMEM,
        scratch_shapes=[acc],
        compiler_params=params,
        name="tiles",
    )

    def settled(value):
        return lax.optimization_barrier((value, value.astype(jnp.bfloat16)))

    t1, field_1 = settled(t1)
    t2 = 2.0 * reduce(following(table, gather(field_1), held, others)) - field.astype(jnp.float32)
    t2, field_2 = settled(t2)
    t3 = 2.0 * reduce(following(table, gather(field_2), held, others)) - t1
    t3, field_3 = settled(t3)

    part, base, scale = pl.pallas_call(
        last_kernel,
        out_shape=(partial, plane, plane),
        in_specs=[SMEM, SMEM] + [VMEM] * 7,
        out_specs=(VMEM, VMEM, VMEM),
        scratch_shapes=[acc],
        compiler_params=params,
        name="last",
    )(table, coefficients, gather(field_3), held, others, field, t1, t2, t3)
    heat = base + scale * reduce(part)

    mine = jnp.where(first, heat[0], heat[1])
    its = lax.ppermute(jnp.where(first, heat[1], heat[0]), "c", SWAP)
    return ordered(mine, its).reshape(2 * half, TILE)


def solution(mesh):
    physical = Mesh(mesh.devices.reshape(SIZES), AXES)
    row, col = AXES[:2], AXES[2:]
    return jax.shard_map(
        on_device,
        mesh=physical,
        in_specs=(
            P(None, AXES),
            P(row, col, None, None, None),
            P(row, col, None, None),
            P(row, col),
            P(),
        ),
        out_specs=P(None, AXES),
        check_vma=False,
    )
```

```python
import jax
import jax.numpy as jnp
from jax import lax
from jax.experimental import pallas as pl
from jax.experimental.pallas import tpu as pltpu
from jax.sharding import Mesh, PartitionSpec as P

TILE = 512
AXES = ("x", "zl", "y", "zh", "c")
SIZES = (4, 4, 4, 4, 2)
SMEM = pl.BlockSpec(memory_space=pltpu.SMEM)
VMEM = pl.BlockSpec(memory_space=pltpu.VMEM)
SWAP = [(0, 1), (1, 0)]
ROW, COL, COUNT, CORE, NOTE = 0, 1, 2, 3, 4


def add_tiles(table_ref, panel_ref, groups, partial_ref, acc_ref):
    acc_ref[...] = jnp.zeros_like(acc_ref)
    for note, slots, tile_of in groups:
        parity = table_ref[note + CORE, 0]
        for slot in range(slots):
            row = table_ref[note + ROW, slot]
            col = table_ref[note + COL, slot]
            picked = panel_ref[col % SIZES[1], col // SIZES[1], parity]
            picked = jnp.where(slot < table_ref[note + COUNT, 0], picked, jnp.zeros_like(picked))
            acc_ref[row] += lax.dot_general(
                picked, tile_of(slot), (((1,), (1,)), ((), ())), preferred_element_type=jnp.float32
            )
    partial_ref[...] = acc_ref[...].astype(jnp.bfloat16)


def spread_kernel(core_ref, keep_ref, arrived_ref, own_ref, t0_ref, copies_ref):
    core = core_ref[0]
    t0_ref[core] = keep_ref[...]
    t0_ref[1 - core] = arrived_ref[: keep_ref.shape[0]]
    for group in range(copies_ref.shape[0]):
        copies_ref[group] = t0_ref[...]


def tile_kernel(table_ref, panel_ref, own_ref, other_ref, partial_ref, acc_ref):
    slots = own_ref.shape[0]
    groups = (NOTE, slots, lambda slot: other_ref[slot]), (0, slots, lambda slot: own_ref[slot])
    add_tiles(table_ref, panel_ref, groups, partial_ref, acc_ref)


def last_kernel(
    table_ref,
    weight_ref,
    panel_ref,
    own_ref,
    other_ref,
    t0_ref,
    t1_ref,
    t2_ref,
    t3_ref,
    partial_ref,
    base_ref,
    scale_ref,
    acc_ref,
):
    base_ref[...] = (
        weight_ref[0] * t0_ref[...].astype(jnp.float32)
        + weight_ref[1] * t1_ref[...]
        + (weight_ref[2] - weight_ref[4]) * t2_ref[...]
        + weight_ref[3] * t3_ref[...]
    )
    scale_ref[...] = jnp.full(scale_ref.shape, 2.0 * weight_ref[4], jnp.float32)
    tile_kernel(table_ref, panel_ref, own_ref, other_ref, partial_ref, acc_ref)


def on_device(probes, tiles, tile_index, tile_count, coefficients):
    slabs = tiles[0, 0]
    half = probes.shape[0] // 2
    core = lax.axis_index("c").astype(jnp.int32)
    first = core == 0

    def ordered(mine, its):
        return jnp.where(first, jnp.stack([mine, its]), jnp.stack([its, mine]))

    keep = jnp.where(first, probes[:half], probes[half:])
    give = jnp.where(first, probes[half:], probes[:half])
    slots = slabs.shape[0]
    note = jnp.concatenate(
        [
            tile_index[0, 0].T,
            jnp.broadcast_to(tile_count, (1, slots)),
            jnp.broadcast_to(core, (1, slots)),
        ]
    ).astype(jnp.bfloat16)
    send = jnp.concatenate([give, jnp.pad(note, ((0, half - NOTE), (0, TILE - slots)))])
    send = lax.optimization_barrier(send)
    arrived = lax.ppermute(send, "c", SWAP)
    notes = [both[half : half + NOTE, :slots] for both in (send, arrived)]
    table = jnp.concatenate(notes).astype(jnp.int32)
    params = pltpu.CompilerParams(vmem_limit_bytes=4 * 1024 * 1024)
    groups = SIZES[1] * SIZES[0]
    field, copies = pl.pallas_call(
        spread_kernel,
        out_shape=tuple(jax.ShapeDtypeStruct(more + (2, half, TILE), jnp.bfloat16) for more in ((), (groups,))),
        in_specs=[SMEM, VMEM, VMEM, pl.BlockSpec(memory_space=pltpu.HBM)],
        out_specs=(VMEM, VMEM),
        compiler_params=params,
        name="spread",
    )(core.reshape(1), keep, arrived, pltpu.with_memory_space_constraint(slabs, pltpu.HBM))
    copies, table, slabs = lax.optimization_barrier((copies, table, slabs))
    others = lax.ppermute(slabs, "c", SWAP)

    rows = SIZES[2] * SIZES[3] * SIZES[4]
    partial = jax.ShapeDtypeStruct((rows, half, TILE), jnp.bfloat16)
    plane = jax.ShapeDtypeStruct((2, half, TILE), jnp.float32)
    acc = pltpu.VMEM(partial.shape, jnp.float32)

    def exchange(copies):
        panel = lax.all_to_all(copies, ("zl", "x"), 0, 0, tiled=True)
        return panel.reshape((SIZES[1], SIZES[0]) + copies.shape[1:])

    def gather(field_bf):
        return exchange(jnp.broadcast_to(field_bf[None], (groups,) + field_bf.shape))

    def total(parts, axis):
        arrived = lax.all_to_all(parts, axis, 0, 0, tiled=True)
        a, b, c, d = (arrived[k].astype(jnp.float32) for k in range(4))
        return (a + b) + (c + d)

    def reduce(part):
        along_y = total(part.reshape(SIZES[2], -1, half, TILE), "y").astype(jnp.bfloat16)
        return total(along_y.reshape(SIZES[3], 2, half, TILE), "zh")

    following = pl.pallas_call(
        tile_kernel,
        out_shape=partial,
        in_specs=[SMEM, VMEM, VMEM, VMEM],
        out_specs=VMEM,
        scratch_shapes=[acc],
        compiler_params=params,
        name="tiles",
    )
    t1 = reduce(following(table, exchange(copies), slabs, others))

    def settled(value):
        return lax.optimization_barrier((value, value.astype(jnp.bfloat16)))

    t1, field_1 = settled(t1)
    t2 = 2.0 * reduce(following(table, gather(field_1), slabs, others)) - field.astype(jnp.float32)
    t2, field_2 = settled(t2)
    t3 = 2.0 * reduce(following(table, gather(field_2), slabs, others)) - t1
    t3, field_3 = settled(t3)

    part, base, scale = pl.pallas_call(
        last_kernel,
        out_shape=(partial, plane, plane),
        in_specs=[SMEM, SMEM] + [VMEM] * 7,
        out_specs=(VMEM, VMEM, VMEM),
        scratch_shapes=[acc],
        compiler_params=params,
        name="last",
    )(table, coefficients, gather(field_3), slabs, others, field, t1, t2, t3)
    heat = base + scale * reduce(part)

    mine = jnp.where(first, heat[0], heat[1])
    its = lax.ppermute(jnp.where(first, heat[1], heat[0]), "c", SWAP)
    return ordered(mine, its).reshape(2 * half, TILE)


def solution(mesh):
    physical = Mesh(mesh.devices.reshape(SIZES), AXES)
    row, col = AXES[:2], AXES[2:]
    return jax.shard_map(
        on_device,
        mesh=physical,
        in_specs=(
            P(None, AXES),
            P(row, col, None, None, None),
            P(row, col, None, None),
            P(row, col),
            P(),
        ),
        out_specs=P(None, AXES),
        check_vma=False,
    )
```

```python
import jax
import jax.numpy as jnp
from jax import lax
from jax.experimental import pallas as pl
from jax.experimental.pallas import tpu as pltpu
from jax.sharding import Mesh, PartitionSpec as P

TILE = 512
AXES = ("x", "zl", "y", "zh", "c")
SIZES = (4, 4, 4, 4, 2)
SMEM = pl.BlockSpec(memory_space=pltpu.SMEM)
VMEM = pl.BlockSpec(memory_space=pltpu.VMEM)
SWAP = [(0, 1), (1, 0)]
ROW, COL, COUNT, CORE, NOTE = 0, 1, 2, 3, 4


def first_kernel(index_ref, count_ref, core_ref, probes_ref, panel_ref, own_ref, mine_ref, theirs_ref, acc_ref):
    acc_ref[...] = jnp.zeros_like(acc_ref)
    slots = own_ref.shape[0]
    count, core = count_ref[0], core_ref[0]
    for slot in range(slots):
        row, col = index_ref[ROW, slot], index_ref[COL, slot]
        picked = panel_ref[col % SIZES[1], col // SIZES[1]]
        picked = jnp.where(slot < count, picked, jnp.zeros_like(picked))
        acc_ref[row] += lax.dot_general(
            picked, own_ref[slot], (((1,), (1,)), ((), ())), preferred_element_type=jnp.float32
        )
    rows, half = acc_ref.shape[0], mine_ref.shape[1]
    for out_ref, which in ((mine_ref, core), (theirs_ref, 1 - core)):
        columns = pl.ds(pl.multiple_of(which * half, half), half)
        out_ref[:rows] = acc_ref[:, columns].astype(jnp.bfloat16)
        out_ref[rows] = probes_ref[columns]
    shape = (half, 128)
    line, lane = lax.broadcasted_iota(jnp.int32, shape, 0), lax.broadcasted_iota(jnp.int32, shape, 1)
    note = jnp.where(line == COUNT, count, jnp.where(line == CORE, core, 0))
    for slot in range(slots):
        place = jnp.where(line == ROW, index_ref[ROW, slot], index_ref[COL, slot])
        note = jnp.where((lane == slot) & (line <= COL), place, note)
    theirs_ref[rows + 1] = jnp.zeros(theirs_ref.shape[1:], jnp.bfloat16)
    theirs_ref[rows + 1, :, :128] = note.astype(jnp.float32).astype(jnp.bfloat16)


def spread_kernel(probes_hbm, index_hbm, own_ref, copies_ref, kept_ref, index_ref, sems):
    fetch_probes = pltpu.make_async_copy(probes_hbm, kept_ref, sems.at[0])
    fetch_index = pltpu.make_async_copy(index_hbm, index_ref, sems.at[1])
    fetch_probes.start()
    fetch_index.start()
    fetch_probes.wait()
    for group in range(copies_ref.shape[0]):
        copies_ref[group] = kept_ref[...]
    fetch_index.wait()


def tile_kernel(table_ref, panel_ref, own_ref, other_ref, partial_ref, acc_ref):
    acc_ref[...] = jnp.zeros_like(acc_ref)
    for tiles_ref, note in ((own_ref, 0), (other_ref, NOTE)):
        parity = table_ref[note + CORE, 0]
        for slot in range(own_ref.shape[0]):
            row = table_ref[note + ROW, slot]
            col = table_ref[note + COL, slot]
            picked = panel_ref[col % SIZES[1], col // SIZES[1], parity]
            picked = jnp.where(slot < table_ref[note + COUNT, 0], picked, jnp.zeros_like(picked))
            acc_ref[row] += lax.dot_general(
                picked, tiles_ref[slot], (((1,), (1,)), ((), ())), preferred_element_type=jnp.float32
            )
    partial_ref[...] = acc_ref[...].astype(jnp.bfloat16)


def last_kernel(
    table_ref,
    weight_ref,
    panel_ref,
    own_ref,
    other_ref,
    t0_ref,
    t1_ref,
    t2_ref,
    t3_ref,
    partial_ref,
    base_ref,
    scale_ref,
    acc_ref,
):
    base_ref[...] = (
        weight_ref[0] * t0_ref[...].astype(jnp.float32)
        + weight_ref[1] * t1_ref[...]
        + (weight_ref[2] - weight_ref[4]) * t2_ref[...]
        + weight_ref[3] * t3_ref[...]
    )
    scale_ref[...] = jnp.full(scale_ref.shape, 2.0 * weight_ref[4], jnp.float32)
    tile_kernel(table_ref, panel_ref, own_ref, other_ref, partial_ref, acc_ref)


def on_device(probes, tiles, tile_index, tile_count, coefficients):
    slabs = tiles[0, 0]
    half = probes.shape[0] // 2
    slots = slabs.shape[0]
    core = lax.axis_index("c").astype(jnp.int32)
    first = core == 0
    index = tile_index[0, 0].T
    count = jnp.minimum(tile_count[0], slots)
    core, first, count = lax.optimization_barrier((core, first, count))
    params = pltpu.CompilerParams(vmem_limit_bytes=4 * 1024 * 1024)
    groups = SIZES[1] * SIZES[0]
    copies, probes, index = pl.pallas_call(
        spread_kernel,
        out_shape=(
            jax.ShapeDtypeStruct((groups,) + probes.shape, probes.dtype),
            jax.ShapeDtypeStruct(probes.shape, probes.dtype),
            jax.ShapeDtypeStruct(index.shape, index.dtype),
        ),
        in_specs=[pl.BlockSpec(memory_space=pltpu.HBM)] * 3,
        out_specs=(VMEM, VMEM, VMEM),
        scratch_shapes=[pltpu.SemaphoreType.DMA((2,))],
        compiler_params=params,
        name="spread",
    )(*(pltpu.with_memory_space_constraint(value, pltpu.HBM) for value in (probes, index, slabs)))
    copies, core, count = lax.optimization_barrier((copies, core, count))

    def ordered(mine, its):
        return jnp.where(first, jnp.stack([mine, its]), jnp.stack([its, mine]))

    rows = SIZES[2] * SIZES[3] * SIZES[4]
    partial = jax.ShapeDtypeStruct((rows, half, TILE), jnp.bfloat16)
    plane = jax.ShapeDtypeStruct((2, half, TILE), jnp.float32)
    acc = pltpu.VMEM(partial.shape, jnp.float32)

    def exchange(copies):
        panel = lax.all_to_all(copies, ("zl", "x"), 0, 0, tiled=True)
        return panel.reshape((SIZES[1], SIZES[0]) + copies.shape[1:])

    def gather(field_bf):
        return exchange(jnp.broadcast_to(field_bf[None], (groups,) + field_bf.shape))

    def total(parts, axis):
        arrived = lax.all_to_all(parts, axis, 0, 0, tiled=True)
        a, b, c, d = (arrived[k].astype(jnp.float32) for k in range(4))
        return (a + b) + (c + d)

    def reduce(part):
        along_y = total(part.reshape(SIZES[2], -1, half, TILE), "y").astype(jnp.bfloat16)
        return total(along_y.reshape(SIZES[3], 2, half, TILE), "zh")

    mine, theirs = pl.pallas_call(
        first_kernel,
        out_shape=tuple(jax.ShapeDtypeStruct((rows + more, half, TILE), jnp.bfloat16) for more in (1, 2)),
        in_specs=[SMEM, SMEM, SMEM, VMEM, VMEM, VMEM],
        out_specs=(VMEM, VMEM),
        scratch_shapes=[pltpu.VMEM((rows, 2 * half, TILE), jnp.float32)],
        compiler_params=params,
        name="first",
    )(index, count, core.reshape(1), probes, exchange(copies), slabs)
    arrived = lax.ppermute(theirs, "c", SWAP)
    part = (mine[:rows].astype(jnp.float32) + arrived[:rows].astype(jnp.float32)).astype(jnp.bfloat16)
    field = ordered(mine[rows], arrived[rows])
    table = jnp.concatenate([both[rows + 1, :NOTE, :slots] for both in (theirs, arrived)]).astype(jnp.int32)
    part, field, table, slabs = lax.optimization_barrier((part, field, table, slabs))
    others = lax.ppermute(slabs, "c", SWAP)
    t1 = reduce(part)
    following = pl.pallas_call(
        tile_kernel,
        out_shape=partial,
        in_specs=[SMEM, VMEM, VMEM, VMEM],
        out_specs=VMEM,
        scratch_shapes=[acc],
        compiler_params=params,
        name="tiles",
    )

    def settled(value):
        return lax.optimization_barrier((value, value.astype(jnp.bfloat16)))

    t1, field_1 = settled(t1)
    t2 = 2.0 * reduce(following(table, gather(field_1), slabs, others)) - field.astype(jnp.float32)
    t2, field_2 = settled(t2)
    t3 = 2.0 * reduce(following(table, gather(field_2), slabs, others)) - t1
    t3, field_3 = settled(t3)

    part, base, scale = pl.pallas_call(
        last_kernel,
        out_shape=(partial, plane, plane),
        in_specs=[SMEM, SMEM] + [VMEM] * 7,
        out_specs=(VMEM, VMEM, VMEM),
        scratch_shapes=[acc],
        compiler_params=params,
        name="last",
    )(table, coefficients, gather(field_3), slabs, others, field, t1, t2, t3)
    heat = base + scale * reduce(part)

    mine = jnp.where(first, heat[0], heat[1])
    its = lax.ppermute(jnp.where(first, heat[1], heat[0]), "c", SWAP)
    return ordered(mine, its).reshape(2 * half, TILE)


def solution(mesh):
    physical = Mesh(mesh.devices.reshape(SIZES), AXES)
    row, col = AXES[:2], AXES[2:]
    return jax.shard_map(
        on_device,
        mesh=physical,
        in_specs=(
            P(None, AXES),
            P(row, col, None, None, None),
            P(row, col, None, None),
            P(row, col),
            P(),
        ),
        out_specs=P(None, AXES),
        check_vma=False,
    )
```
